32 devices in a mesh: dp: 8 (over z, core), tensor: 4 (over y, x).
Axes of the slice: x: 2, y: 2, z: 4, core: 2. Of those that a mesh axis runs over, the one named last changes fastest.
Arguments:
- inputs: bfloat16 [5832, 1152], P('dp'), may hold values from -6 to 6
- cotangent: bfloat16 [5832, 1152], P('dp'), may hold values from -6 to 6
- ln1_gain: float32 [1152], replicated, may hold values from 0.1 to 1.9
- ln1_shift: float32 [1152], replicated, may hold values from -3 to 3
- w_qkv: bfloat16 [1152, 3, 1152], P(None, None, 'tensor'), may hold values from -0.1875 to 0.1875
- bias_qv: float32 [2, 1152], P(None, 'tensor'), may hold values from -3 to 3
- w_out: bfloat16 [1152, 1152], P('tensor'), may hold values from -3 to 3
- bias_out: float32 [1152], replicated, may hold values from -3 to 3
- ln2_gain: float32 [1152], replicated, may hold values from 0.1 to 1.9
- ln2_shift: float32 [1152], replicated, may hold values from -3 to 3
- w_up: bfloat16 [1152, 4304], P(None, 'tensor'), may hold values from -1 to 1
- bias_up: float32 [4304], P('tensor'), may hold values from -3 to 3
- w_down: bfloat16 [4304, 1152], P('tensor'), may hold values from -0.25 to 0.25
- bias_down: float32 [1152], replicated, may hold values from -3 to 3
Outputs:
- layer_output: bfloat16 [5832, 1152], P('dp', 'tensor')
- input_grad: float32 [5832, 1152], P('dp', 'tensor')
- grad_ln1_gain: float32 [1152], replicated
- grad_ln1_shift: float32 [1152], replicated
- grad_w_qkv: float32 [1152, 3, 1152], P(None, None, 'tensor')
- grad_bias_qv: float32 [2, 1152], P(None, 'tensor')
- grad_w_out: float32 [1152, 1152], P('tensor')
- grad_bias_out: float32 [1152], replicated
- grad_ln2_gain: float32 [1152], replicated
- grad_ln2_shift: float32 [1152], replicated
- grad_w_up: float32 [1152, 4304], P(None, 'tensor')
- grad_bias_up: float32 [4304], P('tensor')
- grad_w_down: float32 [4304, 1152], P('tensor')
- grad_bias_down: float32 [1152], replicated
The draws below stay inside these ranges and needn't reach their ends.
All inputs are finite; a program needn't handle non-finite values.
Results may differ from the reference program's by a relative error of at most 0.028.
Values may be sent and summed in bfloat16 or wider, within the bound.
No kernel may reach another device: no remote copies, remote signals or barrier semaphores. Data moves between devices by JAX's collectives and lax.ppermute only.
A program may use at most 128 MiB of HBM per device.

```python
import jax
import jax.numpy as jnp
from jax import lax

D = 1152
HEADS = 16
HEAD_DIM = 72
FF = 4304
SEQ = 729
IMAGES = 8
TOKENS = 5832
N_TENSOR = 4


def draw_w_up(key, part):
    noise_key, column_key = jax.random.split(jax.random.fold_in(key, 17))
    noise = jnp.clip(jax.random.normal(noise_key, (D, FF), jnp.float32), -5.0, 5.0)
    column_part = jnp.clip(jax.random.normal(column_key, (1, FF), jnp.float32), -5.0, 5.0)
    return ((noise + column_part) * (2.0 * D) ** (-0.5)).astype(jnp.bfloat16)


def levels(key, shape, shards, smallest, top_value):
    factor_of = 1.0
    for axis_at, blocks in shards:
        draws = jax.random.uniform(jax.random.fold_in(jax.random.fold_in(key, 6), axis_at), (blocks,), jnp.float32, smallest / len(shards), top_value / len(shards))
        factor_of = factor_of * jnp.repeat(jnp.exp(draws), shape[axis_at] // blocks).reshape((-1,) + (1,) * (len(shape) - 1 - axis_at))
    return factor_of


def normal_values(stream_key, extent, deviation, most, cuts=(), dtype=jnp.bfloat16):
    factor_of = levels(stream_key, extent, cuts, -0.22, 0.18) if cuts else 1.0
    drawn = jax.random.normal(stream_key, extent, jnp.float32) * deviation * factor_of
    return jnp.minimum(jnp.maximum(drawn, -most), most).astype(dtype)


def setup_inputs(seed: int = 0) -> dict:
    key_of = jax.random.split(jax.random.key(seed), 15)
    return {
        "inputs": normal_values(key_of[0], (TOKENS, D), 1.0, 6.0, ((0, 8),)),
        "cotangent": normal_values(key_of[1], (TOKENS, D), 1.0, 6.0, ((0, 8),)),
        "ln1_gain": jnp.clip(1.0 + 0.18 * jax.random.normal(key_of[2], (D,), jnp.float32), 0.1, 1.9),
        "ln1_shift": normal_values(key_of[3], (D,), 0.5, 3.0, (), jnp.float32),
        "w_qkv": normal_values(key_of[4], (D, 3, D), D ** -0.5, 0.1875, ((2, 4),)),
        "bias_qv": normal_values(key_of[5], (2, D), 0.5, 3.0, ((1, 4),), jnp.float32),
        "w_out": normal_values(key_of[6], (D, D), (max(D // 288, 1)) ** -0.5, 3.0, ((0, 4),)),
        "bias_out": normal_values(key_of[7], (D,), 0.5, 3.0, (), jnp.float32),
        "ln2_gain": jnp.clip(1.0 + 0.18 * jax.random.normal(key_of[8], (D,), jnp.float32), 0.1, 1.9),
        "ln2_shift": normal_values(key_of[9], (D,), 0.5, 3.0, (), jnp.float32),
        "w_up": draw_w_up(jax.random.fold_in(key_of[14], 71), 0),
        "bias_up": normal_values(key_of[11], (FF,), 0.5, 3.0, ((0, 4),), jnp.float32),
        "w_down": normal_values(key_of[12], (FF, D), (max(FF // 8, 1)) ** -0.5, 0.25, ((0, 4),)),
        "bias_down": normal_values(key_of[13], (D,), 0.5, 3.0, (), jnp.float32),
    }


EPSILON = 1e-06
GELU_C = 0.7978845608028654
GELU_A = 0.044715

def gelu_parts(pre_act):
    inner = GELU_C * (pre_act + GELU_A * pre_act * pre_act * pre_act)
    tangent = jnp.tanh(inner)
    values = 0.5 * pre_act * (1.0 + tangent)
    slopes = 0.5 * (1.0 + tangent) + 0.5 * pre_act * (1.0 - tangent * tangent) * GELU_C * (1.0 + 3.0 * GELU_A * pre_act * pre_act)
    return (values, slopes)

def norm_forward(rows_float, gain, shift):
    average = lax.optimization_barrier(jnp.mean(rows_float, axis=-1, keepdims=True))
    variance = lax.optimization_barrier(jnp.mean(rows_float * rows_float, axis=-1, keepdims=True)) - average * average
    inv_std = lax.rsqrt(variance + EPSILON)
    centred = (rows_float - average) * inv_std
    return (centred, inv_std, centred * gain + shift)

def norm_backward(grad_norm, centred, inv_std, gain):
    grad_hat = grad_norm * gain
    return inv_std * (grad_hat - lax.optimization_barrier(jnp.mean(grad_hat, axis=-1, keepdims=True)) - centred * lax.optimization_barrier(jnp.mean(grad_hat * centred, axis=-1, keepdims=True)))

def grouped_sum(left, right, groups):
    rows = left.shape[0]
    inner = left.shape[1] // groups
    left_group = left.reshape(rows, groups, inner).astype(jnp.float32)
    right_group = right.reshape(groups, inner, right.shape[1]).astype(jnp.float32)
    pieces = jnp.einsum('sgk,gkn->gsn', left_group, right_group).astype(jnp.bfloat16)
    pieces = lax.optimization_barrier(pieces)
    return lax.optimization_barrier(jnp.sum(pieces.astype(jnp.float32), axis=0))

def attend(queries, keys_b, values_b, scaling):
    scores = jnp.einsum('qhd,khd->hqk', queries.astype(jnp.float32), keys_b.astype(jnp.float32)) * scaling
    log_total = jnp.log(lax.optimization_barrier(jnp.sum(jnp.exp(scores), axis=-1, keepdims=True)))
    probs = jnp.exp(scores - log_total).astype(jnp.bfloat16)
    context = jnp.einsum('hqk,khd->qhd', probs.astype(jnp.float32), values_b.astype(jnp.float32)).astype(jnp.bfloat16)
    return (context, log_total)

def attend_back(queries, keys_b, values_b, context, log_total, grad_ctx, scaling):
    query_float = queries.astype(jnp.float32)
    key_float = keys_b.astype(jnp.float32)
    grad_float = grad_ctx.astype(jnp.float32)
    scores = jnp.einsum('qhd,khd->hqk', query_float, key_float) * scaling
    probs = jnp.exp(scores - log_total)
    probs_b = probs.astype(jnp.bfloat16)
    delta = lax.optimization_barrier(jnp.sum(grad_float * context.astype(jnp.float32), axis=-1))
    along = jnp.einsum('qhd,khd->hqk', grad_float, values_b.astype(jnp.float32))
    grad_scores = (probs * (along - delta.T[:, :, None])).astype(jnp.bfloat16)
    grad_values = jnp.einsum('hqk,qhd->khd', probs_b.astype(jnp.float32), grad_float)
    grad_queries = jnp.einsum('hqk,khd->qhd', grad_scores.astype(jnp.float32), key_float) * scaling
    grad_keys = jnp.einsum('hqk,qhd->khd', grad_scores.astype(jnp.float32), query_float) * scaling
    return (grad_queries, grad_keys, grad_values)

def reference(inputs, cotangent, ln1_gain, ln1_shift, w_qkv, bias_qv, w_out, bias_out, ln2_gain, ln2_shift, w_up, bias_up, w_down, bias_down):
    groups = N_TENSOR
    scaling = HEAD_DIM ** (-0.5)
    share = D // groups
    right_qkv = w_qkv.reshape(D, 3, groups, share).transpose(2, 1, 3, 0).reshape(3 * D, D)

    def one_image(totals, couple):
        image_in, image_grad = couple
        in_float = image_in.astype(jnp.float32)
        centred_one, inv_one, normed_one = norm_forward(in_float, ln1_gain, ln1_shift)
        first_in = normed_one.astype(jnp.bfloat16)
        project = jnp.einsum('sd,djk->sjk', first_in.astype(jnp.float32), w_qkv.astype(jnp.float32))
        queries = (project[:, 0] + bias_qv[0]).astype(jnp.bfloat16)
        keys_b = project[:, 1].astype(jnp.bfloat16)
        values_b = (project[:, 2] + bias_qv[1]).astype(jnp.bfloat16)
        heads_shape = (SEQ, HEADS, HEAD_DIM)
        context, log_total = attend(queries.reshape(heads_shape), keys_b.reshape(heads_shape), values_b.reshape(heads_shape), scaling)
        context_flat = context.reshape(SEQ, D)
        resid = in_float + grouped_sum(context_flat, w_out, groups) + bias_out
        centred_two, inv_two, normed_two = norm_forward(resid, ln2_gain, ln2_shift)
        second_in = normed_two.astype(jnp.bfloat16)
        pre_act = jnp.dot(second_in, w_up, preferred_element_type=jnp.float32) + bias_up
        gelu_vals, gelu_slopes = gelu_parts(pre_act)
        hidden = gelu_vals.astype(jnp.bfloat16)
        output_rows = (resid + grouped_sum(hidden, w_down, groups) + bias_down).astype(jnp.bfloat16)
        grad_float = image_grad.astype(jnp.float32)
        grad_down = jnp.dot(hidden.T, image_grad, preferred_element_type=jnp.float32)
        grad_bias_down = lax.optimization_barrier(jnp.sum(grad_float, axis=0))
        grad_pre = jnp.dot(image_grad, w_down.T, preferred_element_type=jnp.float32) * gelu_slopes
        grad_pre_b = grad_pre.astype(jnp.bfloat16)
        grad_up = jnp.dot(second_in.T, grad_pre_b, preferred_element_type=jnp.float32)
        grad_bias_up = lax.optimization_barrier(jnp.sum(grad_pre, axis=0))
        back_two = grouped_sum(grad_pre_b, w_up.T, groups)
        grad_gain_two = lax.optimization_barrier(jnp.sum(back_two * centred_two, axis=0))
        grad_shift_two = lax.optimization_barrier(jnp.sum(back_two, axis=0))
        resid_grad = grad_float + norm_backward(back_two, centred_two, inv_two, ln2_gain)
        resid_grad_b = resid_grad.astype(jnp.bfloat16)
        grad_out = jnp.dot(context_flat.T, resid_grad_b, preferred_element_type=jnp.float32)
        grad_bias_out = lax.optimization_barrier(jnp.sum(resid_grad, axis=0))
        grad_ctx = jnp.dot(resid_grad_b, w_out.T, preferred_element_type=jnp.float32).astype(jnp.bfloat16)
        grad_queries, grad_keys, grad_values = attend_back(queries.reshape(heads_shape), keys_b.reshape(heads_shape), values_b.reshape(heads_shape), context, log_total, grad_ctx.reshape(heads_shape), scaling)
        grad_queries = grad_queries.reshape(SEQ, D)
        grad_values = grad_values.reshape(SEQ, D)
        grad_qkv = jnp.stack([grad_queries, grad_keys.reshape(SEQ, D), grad_values], axis=1).astype(jnp.bfloat16)
        grad_wqkv = jnp.einsum('sd,sjk->djk', first_in.astype(jnp.float32), grad_qkv.astype(jnp.float32))
        grad_bias_qv = jnp.stack([lax.optimization_barrier(jnp.sum(grad_queries, axis=0)), lax.optimization_barrier(jnp.sum(grad_values, axis=0))], axis=0)
        left_qkv = grad_qkv.reshape(SEQ, 3, groups, share).transpose(0, 2, 1, 3).reshape(SEQ, 3 * D)
        back_one = grouped_sum(left_qkv, right_qkv, groups)
        grad_gain_one = lax.optimization_barrier(jnp.sum(back_one * centred_one, axis=0))
        grad_shift_one = lax.optimization_barrier(jnp.sum(back_one, axis=0))
        input_rows = resid_grad + norm_backward(back_one, centred_one, inv_one, ln1_gain)
        fresh = (grad_gain_one, grad_shift_one, grad_wqkv, grad_bias_qv, grad_out, grad_bias_out, grad_gain_two, grad_shift_two, grad_up, grad_bias_up, grad_down, grad_bias_down)
        totals = tuple((old + new for old, new in zip(totals, fresh)))
        return (totals, (output_rows, input_rows))
    zeros = (jnp.zeros((D,), jnp.float32), jnp.zeros((D,), jnp.float32), jnp.zeros((D, 3, D), jnp.float32), jnp.zeros((2, D), jnp.float32), jnp.zeros((D, D), jnp.float32), jnp.zeros((D,), jnp.float32), jnp.zeros((D,), jnp.float32), jnp.zeros((D,), jnp.float32), jnp.zeros((D, FF), jnp.float32), jnp.zeros((FF,), jnp.float32), jnp.zeros((FF, D), jnp.float32), jnp.zeros((D,), jnp.float32))
    totals, (output_all, input_all) = lax.scan(one_image, zeros, (inputs.reshape(IMAGES, SEQ, D), cotangent.reshape(IMAGES, SEQ, D)))
    layer_output = output_all.reshape(TOKENS, D)
    input_grad = input_all.reshape(TOKENS, D)
    return (layer_output, input_grad, totals[0], totals[1], totals[2], totals[3], totals[4], totals[5], totals[6], totals[7], totals[8], totals[9], totals[10], totals[11])
```

```python
import jax
import jax.numpy as jnp
import numpy as np
from jax import lax
from jax.experimental import pallas as pl
from jax.experimental.pallas import tpu as pltpu
from jax.sharding import PartitionSpec as P

HEAD_DIM = 72
EPSILON = 1e-06
GELU_C = 0.7978845608028654
GELU_A = 0.044715
LOG2_E = 1.4426950408889634
TENSOR, DP = "tensor", "dp"
F32 = jnp.float32
BF16 = jnp.bfloat16
LANES = 256
MIDDLE_LANES = 384


LAG = 3


def gelu_parts(pre_act):
    square = pre_act * pre_act
    tangent = jnp.tanh(pre_act * (GELU_C + GELU_C * GELU_A * square))
    half = 0.5 + 0.5 * tangent
    values = pre_act * half
    slopes = half + (values - values * tangent) * (GELU_C + 3.0 * GELU_C * GELU_A * square)
    return (values, slopes)


def norm_parts(rows_float):
    width = rows_float.shape[-1]
    average = jnp.sum(rows_float, axis=-1, keepdims=True) / width
    variance = jnp.sum(rows_float * rows_float, axis=-1, keepdims=True) / width - average * average
    inv_std = lax.rsqrt(variance + EPSILON)
    return ((rows_float - average) * inv_std, inv_std)


def dot(left, right, over):
    return lax.dot_general(left, right, (((over[0],), (over[1],)), ((), ())), preferred_element_type=F32)


def masked(ref, tokens):
    rows = ref.shape[0]
    at = pl.program_id(0) * rows + lax.broadcasted_iota(jnp.int32, (rows, 1), 0)
    return jnp.where(at < tokens, ref[...].astype(F32), 0.0)


def as_row(ref):
    return ref[...].reshape(1, -1)


def as_col(row):
    return jnp.broadcast_to(row, (8, row.shape[1])).T[:, 0:1]


def col_as_row(column):
    return jnp.broadcast_to(column, (column.shape[0], 128)).T[0:1]


def struct(shape, dtype):
    return jax.ShapeDtypeStruct(shape, dtype)


def whole(shape):
    return pl.BlockSpec(shape, lambda *_: (0,) * len(shape))


def fixed(shape):
    return pl.BlockSpec(shape, lambda *_: (0,) * len(shape), pipeline_mode=pl.Buffered(1))


def call(body, grid, ins, outs, scratch=(), flops=0, moved=0, limit=24, far=(), near=()):
    shapes, specs = [o[0] for o in outs], [o[1] for o in outs]
    run = pl.pallas_call(
        body,
        out_shape=shapes,
        grid_spec=pltpu.PrefetchScalarGridSpec(
            num_scalar_prefetch=1, grid=grid, in_specs=ins, out_specs=specs, scratch_shapes=scratch
        ),
        compiler_params=pltpu.CompilerParams(vmem_limit_bytes=limit * 1024 * 1024),
        cost_estimate=pl.CostEstimate(flops=flops, bytes_accessed=moved, transcendentals=0),
    )

    def named(*args):
        args = list(args)
        for k in far:
            args[k] = pltpu.with_memory_space_constraint(args[k], pltpu.HBM)
        for k in near:
            args[k] = pltpu.with_memory_space_constraint(args[k], pltpu.VMEM)
        return run(*args)

    return named


def make_local(tensor_size, dp_size):
    line = dp_size // 2
    bits = [1 << k for k in range(tensor_size.bit_length() - 1)]
    routes = [bits[c:] + bits[:c] for c in (0, 1)] if len(bits) > 1 else [bits, bits]
    cores = [(i, i ^ 1) for i in range(dp_size)]

    def gather_order(route):
        order = [0]
        for bit in route:
            order = order + [r ^ bit for r in order]
        return order

    def along_route(array, stage):
        pairs = []
        for d in range(dp_size):
            bit = routes[d % 2][stage]
            pairs += [(d * tensor_size + i, d * tensor_size + (i ^ bit)) for i in range(tensor_size)]
        return lax.ppermute(array, (DP, TENSOR), pairs)

    def to_other_core(array):
        return lax.ppermute(array, DP, cores)

    def swap(array, couples):
        there = {}
        for left, right in couples:
            there[left], there[right] = right, left
        pairs = []
        for p in range(line):
            for c in range(2):
                pairs.append((2 * p + c, 2 * there[p] + c if p in there else 2 * p + 1 - c))
        return lax.ppermute(array, DP, pairs)

    def outward(step):
        return [(step, step + 1), (line - 1 - step, line - 2 - step)]

    middle = [(line // 2 - 1, line // 2)] if line > 1 else []

    def gather(array):
        held = [array]
        for stage in range(len(bits)):
            joined = held[0] if stage == 0 else jnp.concatenate(held, axis=0)
            held.append(along_route(joined, stage))
        return held

    def scatter(pieces):
        pieces = list(pieces)
        rows = pieces[0].shape[0]
        terms = [pieces[0]]
        for stage in range(len(bits)):
            got = along_route(pieces[-1], stage)
            pieces = pieces[:-1]
            terms.append(got)
            start = rows
            for k in range(1, len(pieces)):
                size = pieces[k].shape[0]
                pieces[k] = add_rounded(pieces[k], got[start : start + size])
                start += size
        return terms

    def line_sum(part, place):
        steps = line // 2 - 1
        for i in range(steps):
            part = add_rounded(part, swap(part, outward(i)))
        if middle:
            part = add_rounded(part, swap(part, middle))
        for i in reversed(range(steps)):
            got = swap(part, outward(i))
            part = jnp.where((place == i) | (place == line - 1 - i), got, part)
        return part

    def line_sums(parts, place):
        if line != 4:
            return {name: line_sum(part, place) for name, part in parts.items()}
        outer = (place == 0) | (place == line - 1)
        names = list(parts)
        totals, sums = {}, {}
        for k in range(len(names) + LAG):
            coming = names[k] if k < len(names) else None
            going = names[k - LAG] if k >= LAG else None
            if going is None:
                payload = parts[coming]
            elif coming is None:
                payload = totals[going]
            else:
                back = totals[going]
                rows = parts[coming].shape[0]
                back = jnp.pad(back, ((0, rows - back.shape[0]), (0, 0)))
                payload = jnp.where(outer, parts[coming], back)
            got = swap(payload, outward(0))
            if coming is not None:
                part = add_rounded(parts[coming], got)
                across = swap(part, middle)
                totals[coming] = add_rounded(part, across)
            if going is not None:
                sums[going] = jnp.where(outer, got[: totals[going].shape[0]], totals[going])
        return sums

    def add_rounded(left, right):
        return (left.astype(F32) + right.astype(F32)).astype(BF16)

    def local(
        inputs,
        cotangent,
        ln1_gain,
        ln1_shift,
        w_qkv,
        bias_qv,
        w_out,
        bias_out,
        ln2_gain,
        ln2_shift,
        w_up,
        bias_up,
        w_down,
        bias_down,
    ):
        me = lax.axis_index(TENSOR)
        replica = lax.axis_index(DP)
        core, place = replica % 2, replica // 2
        tokens, width = inputs.shape
        share = width // tensor_size
        hidden_size = w_down.shape[0]
        unit = max(LANES, 16 * tensor_size)
        padded = -(-tokens // unit) * unit
        steps = padded // LANES
        block = padded // tensor_size
        hidden_rows = -(-hidden_size // 64) * 64
        heads = share // HEAD_DIM
        scaling = HEAD_DIM ** (-0.5)
        gathered_at, other_at, scattered_at = 0, tensor_size, 2 * tensor_size
        core_at = 3 * tensor_size
        tables = []
        for c in (0, 1):
            orders = gather_order(routes[c]) + gather_order(routes[1 - c])
            tables.append(np.array(orders + gather_order(routes[c][::-1]) + [0], np.int32))
        scal = jnp.where(core == 0, tables[0], tables[1]) ^ me
        scal = jnp.where(np.arange(core_at + 1) == core_at, core, scal).astype(jnp.int32)
        sizes = [1] + [1 << k for k in range(len(bits))]
        starts = [0] + [1 << k for k in range(len(bits))]

        def block_of(s, index, size):
            return pl.ds(pl.multiple_of(s[index] * size, size), size)

        def place_blocks(s, table, size, refs, target, offset=0, rows=None):
            rows = size if rows is None else rows
            for ref, count, start in zip(refs, sizes, starts):
                for k in range(count):
                    at = s[table + start + k] * size + offset
                    target[pl.ds(pl.multiple_of(at, 16), rows)] = ref[k * rows : (k + 1) * rows]

        w_up_t = w_up.T
        w_qkv_t = w_qkv.transpose(1, 2, 0).reshape(3 * share, width)
        vector = whole((width,))
        rows_in = pl.BlockSpec((LANES, width), lambda i, s: (i, 0))
        lanes_of = lambda n: pl.BlockSpec((n, LANES), lambda i, s: (0, i))

        half_share = share // 2
        w_own = gather(lax.dynamic_slice_in_dim(w_out, core * half_share, half_share, 0))
        w_other = to_other_core(jnp.concatenate(w_own, axis=0))
        w_arrays = len(w_own)

        def project_body(s, x, gain, shift, w, bias, first, qkv):
            centred, _ = norm_parts(masked(x, tokens))
            rounded = (centred * as_row(gain) + as_row(shift)).astype(BF16)
            first[...] = rounded
            projected = dot(w[...], rounded, (1, 1))
            rows = jnp.concatenate([bias[...], jnp.zeros((6, share), F32)], axis=0).T
            qkv[:share] = (projected[:share] + rows[:, 0:1]).astype(BF16)
            qkv[share : 2 * share] = projected[share : 2 * share].astype(BF16)
            qkv[2 * share :] = (projected[2 * share :] + rows[:, 1:2]).astype(BF16)

        first_in, qkv = call(
            project_body,
            (steps,),
            [rows_in, vector, vector, whole((3 * share, width)), whole((2, share))],
            [
                (struct((padded, width), BF16), rows_in),
                (struct((3 * share, padded), BF16), lanes_of(3 * share)),
            ],
            flops=2 * padded * width * 3 * share,
            moved=8_000_000,
            far=(1, 2, 3, 4, 5),
        )(scal, inputs, ln1_gain, ln1_shift, w_qkv_t, bias_qv)
        qkv = qkv.reshape(3, share, padded)

        head3 = pl.BlockSpec((3, HEAD_DIM, padded), lambda h, s: (0, h, 0))
        head1 = pl.BlockSpec((HEAD_DIM, padded), lambda h, s: (h, 0))
        square = pl.BlockSpec((None, padded, padded), lambda h, s: (h, 0, 0))

        def attend_body(s, qkv, context, probs):
            scores = dot(qkv[1], qkv[0], (0, 0)) * (scaling * LOG2_E)
            at = lax.broadcasted_iota(jnp.int32, (padded, 1), 0)
            weights = jnp.where(at < tokens, jnp.exp2(scores), 0.0)
            rounded = (weights * (1.0 / jnp.sum(weights, axis=0, keepdims=True))).astype(BF16)
            probs[...] = rounded
            context[...] = dot(qkv[2], rounded, (1, 0)).astype(BF16)

        context, probs = call(
            attend_body,
            (heads,),
            [head3],
            [
                (struct((share, padded), BF16), head1),
                (pltpu.HBM((heads, padded, padded), BF16), square),
            ],
            flops=8 * padded * padded * 256 * heads,
            moved=8_000_000,
        )(scal, qkv)
        contexts = gather(context)

        def early_body(s, x, cot, w_down, centred_t, inv_t, hidden_grad, cot_padded):
            centred, inv_std = norm_parts(masked(x, tokens))
            centred_t[...] = centred.T.astype(BF16)
            inv_t[...] = jnp.broadcast_to(inv_std, (LANES, 128)).T[:8]
            rounded = masked(cot, tokens).astype(BF16)
            cot_padded[...] = rounded
            hidden_grad[...] = dot(w_down[...], rounded, (1, 1)).astype(BF16)

        centred_t, inv_t, hidden_grad, cot = call(
            early_body,
            (steps,),
            [rows_in, rows_in, whole((hidden_size, width))],
            [
                (struct((width, padded), BF16), lanes_of(width)),
                (struct((8, padded), F32), lanes_of(8)),
                (struct((hidden_size, padded), BF16), lanes_of(hidden_size)),
                (struct((padded, width), BF16), rows_in),
            ],
            flops=2 * padded * width * hidden_size,
            moved=8_000_000,
            far=(1, 2, 3),
        )(scal, inputs, cotangent, w_down)

        def turn_body(s, w_down, w_qkv, down_t, qkv_n):
            down_t[...] = w_down[...].astype(F32).T.astype(BF16)
            qkv_n[...] = w_qkv[...].astype(F32).T.astype(BF16)

        turn_wide = 384
        turn_cols = lambda n: pl.BlockSpec((n, turn_wide), lambda i, s: (0, i))
        turn_rows = lambda n: pl.BlockSpec((turn_wide, n), lambda i, s: (i, 0))
        w_down_t, w_qkv_n = call(
            turn_body,
            (width // turn_wide,),
            [turn_cols(hidden_size), turn_cols(3 * share)],
            [
                (struct((width, hidden_size), BF16), turn_rows(hidden_size)),
                (struct((width, 3 * share), BF16), turn_rows(3 * share)),
            ],
            moved=10_000_000,
            far=(1, 2),
        )(scal, w_down, w_qkv_t)

        mid_lanes = MIDDLE_LANES
        mid_steps = padded // mid_lanes
        mid_rows = pl.BlockSpec((mid_lanes, width), lambda i, s: (i, 0))
        mid_lanes_of = lambda n: pl.BlockSpec((n, mid_lanes), lambda i, s: (0, i))

        def middle_body(s, *refs):
            ctx, refs = refs[:w_arrays], refs[w_arrays:]
            outs, refs = refs[:w_arrays], refs[w_arrays:]
            other, x, b_out, gain, shift, w_up, b_up, grad_in, *refs = refs
            hidden, grad_pre, second, resid, bias_grad, resid_own, *refs = refs
            pieces, (w_all, back_all, resid_all, ctx_all, bias_sum) = refs[:-5], refs[-5:]
            i = pl.program_id(0)

            @pl.when(i == 0)
            def _():
                core_here = s[core_at]
                place_blocks(s, gathered_at, share, outs, w_all, core_here * half_share, half_share)
                for k in range(tensor_size):
                    at = s[other_at + k] * share + (1 - core_here) * half_share
                    rows = other[k * half_share : (k + 1) * half_share]
                    w_all[pl.ds(pl.multiple_of(at, 16), half_share)] = rows
                bias_sum[...] = jnp.zeros_like(bias_sum)

            place_blocks(s, gathered_at, share, ctx, ctx_all)
            total = masked(x, tokens) + dot(ctx_all[...], w_all[...], (0, 0)) + as_row(b_out)
            at = pl.ds(pl.multiple_of(i * mid_lanes, mid_lanes), mid_lanes)
            resid_all[at] = total
            resid[...] = total.astype(BF16)
            centred, _ = norm_parts(total)
            rounded = (centred * as_row(gain) + as_row(shift)).astype(BF16)
            second[...] = rounded
            values, slopes = gelu_parts(dot(w_up[...], rounded, (1, 1)) + as_col(as_row(b_up)))
            hidden[:hidden_size] = values.astype(BF16)
            grad = grad_in[...].astype(F32) * slopes
            bias_sum[...] += jnp.sum(grad, axis=1, keepdims=True)
            grad_b = grad.astype(BF16)
            grad_pre[:hidden_size] = grad_b
            for ref in (hidden, grad_pre):
                ref[hidden_size:] = jnp.zeros((hidden_rows - hidden_size, mid_lanes), BF16)
            back_all[at] = dot(grad_b, w_up[...], (0, 0)).astype(BF16)

            @pl.when(i == mid_steps - 1)
            def _():
                bias_grad[...] = jnp.zeros_like(bias_grad)
                bias_grad[:, :hidden_size] = col_as_row(bias_sum[...])
                resid_own[...] = resid_all[block_of(s, scattered_at, block)]
                for piece, count, start in zip(pieces, sizes, starts):
                    for k in range(count):
                        rows = back_all[block_of(s, scattered_at + start + k, block)]
                        piece[k * block : (k + 1) * block] = rows

        token_block = whole((block, width))
        hidden, grad_pre, second_in, resid, bias_up_grad, resid_own, *back_pieces = call(
            middle_body,
            (mid_steps,),
            [mid_lanes_of(n * share) for n in sizes]
            + [fixed((n * half_share, width)) for n in sizes]
            + [
                fixed((tensor_size * half_share, width)),
                mid_rows,
                vector,
                vector,
                vector,
                fixed((hidden_size, width)),
                whole((hidden_size,)),
                mid_lanes_of(hidden_size),
            ],
            [
                (struct((hidden_rows, padded), BF16), mid_lanes_of(hidden_rows)),
                (struct((hidden_rows, padded), BF16), mid_lanes_of(hidden_rows)),
                (struct((padded, width), BF16), mid_rows),
                (struct((padded, width), BF16), mid_rows),
                (struct((1, width), F32), whole((1, width))),
                (struct((block, width), F32), token_block),
            ]
            + [(struct((n * block, width), BF16), whole((n * block, width))) for n in sizes],
            [
                pltpu.VMEM((width, width), BF16),
                pltpu.VMEM((padded, width), BF16),
                pltpu.VMEM((padded, width), F32),
                pltpu.VMEM((width, mid_lanes), BF16),
                pltpu.VMEM((hidden_size, 1), F32),
            ],
            flops=2 * padded * width * (width + 2 * hidden_size),
            moved=20_000_000,
            limit=36,
            far=(1 + 2 * w_arrays,),
        )(
            scal,
            *contexts,
            *w_own,
            w_other,
            inputs,
            bias_out,
            ln2_gain,
            ln2_shift,
            w_up_t,
            bias_up,
            hidden_grad,
        )
        back_got = scatter(back_pieces)

        chunks = 2
        chunk = -(-hidden_size // (32 * chunks)) * 16
        half = chunk * chunks

        def weight_grad(left, right):
            cols = right.shape[1]
            wide = 384 if cols % 384 == 0 else cols

            def body(s, a, b, *outs):
                for side, which in enumerate((1 - s[core_at], s[core_at])):
                    rows = a[pl.ds(pl.multiple_of(which * half, 16), half)]
                    total = dot(rows, b[...], (1, 0)).astype(BF16)
                    for k in range(chunks):
                        outs[side * chunks + k][...] = total[k * chunk : (k + 1) * chunk]

            outs = call(
                body,
                (cols // wide,),
                [fixed((2 * half, padded)), pl.BlockSpec((padded, wide), lambda i, s: (0, i))],
                [(struct((chunk, cols), BF16), pl.BlockSpec((chunk, wide), lambda i, s: (0, i)))]
                * (2 * chunks),
                flops=2 * hidden_size * padded * cols,
                moved=6_000_000,
            )(scal, left, right)
            return outs

        parts = {}

        def share_with_core(name, other, mine):
            parts[name] = add_rounded(mine, to_other_core(other))

        def by_core(name):
            ours = line_total[name]
            theirs = to_other_core(ours)
            return [jnp.where(core == c, ours, theirs) for c in (0, 1)]

        def dp_sum(name, turned=False):
            sums = [by_core(f"{name}{k}") for k in range(chunks)]
            halves = [pair[c] for c in (0, 1) for pair in sums]
            total = jnp.concatenate(halves, axis=0)[:hidden_size].astype(F32)
            return total.T if turned else total

        for name, cut in (("u", weight_grad(grad_pre, second_in)), ("d", weight_grad(hidden, cot))):
            for k in range(chunks):
                share_with_core(f"{name}{k}", cut[k], cut[chunks + k])

        def norm_body(s, *refs):
            got, (own, cot, gain, grad, sums) = refs[:-5], refs[-5:]
            total = got[0][...].astype(F32)
            for ref in got[1:]:
                total = total + ref[...].astype(F32)
            centred, inv_std = norm_parts(own[...])
            upstream = cot[...].astype(F32)
            hat = total * as_row(gain)
            mean_one = jnp.sum(hat, axis=1, keepdims=True) / width
            mean_two = jnp.sum(hat * centred, axis=1, keepdims=True) / width
            result = upstream + inv_std * (hat - mean_one - centred * mean_two)
            grad[...] = result.astype(BF16)
            total_of = lambda v: jnp.sum(v, axis=0, keepdims=True)
            sums[0:1] = total_of(total * centred)
            sums[1:2] = total_of(total)
            sums[2:3] = total_of(result)
            sums[3:4] = total_of(upstream)

        grad_block, norm_sums = call(
            norm_body,
            (1,),
            [token_block] * len(back_got)
            + [token_block, pl.BlockSpec((block, width), lambda i, s: (s[0], 0)), vector],
            [
                (struct((block, width), BF16), token_block),
                (struct((4, width), F32), whole((4, width))),
            ],
            flops=20 * block * width,
            moved=3_000_000,
        )(scal, *back_got, resid_own, cot, ln2_gain)
        grad_got = gather(grad_block)

        def mlp_body(s, w_down, hidden, *refs):
            pieces, scratch = refs[:-1], refs[-1]
            scratch[...] = dot(w_down[...], hidden[:hidden_size], (1, 0)).astype(BF16)
            for piece, count, start in zip(pieces, sizes, starts):
                for k in range(count):
                    rows = scratch[block_of(s, scattered_at + start + k, share)]
                    piece[k * share : (k + 1) * share] = rows

        mlp_pieces = call(
            mlp_body,
            (steps,),
            [whole((width, hidden_size)), lanes_of(hidden_rows)],
            [(struct((n * share, padded), BF16), lanes_of(n * share)) for n in sizes],
            [pltpu.VMEM((width, LANES), BF16)],
            flops=2 * padded * width * hidden_size,
            moved=6_000_000,
            far=(1, 2),
        )(scal, w_down_t, hidden)
        mlp_got = scatter(mlp_pieces)

        def context_body(s, *refs):
            got, (w, grad_all, grad_ctx) = refs[:-3], refs[-3:]
            place_blocks(s, gathered_at, block, got, grad_all)
            grad_ctx[...] = dot(w[...], grad_all[...], (1, 1)).astype(BF16)

        resid_grad, grad_ctx = call(
            context_body,
            (1,),
            [whole((n * block, width)) for n in sizes] + [whole((share, width))],
            [
                (struct((padded, width), BF16), whole((padded, width))),
                (struct((share, padded), BF16), whole((share, padded))),
            ],
            flops=2 * share * padded * width,
            moved=6_000_000,
        )(scal, *grad_got, w_out)

        def attend_back_body(s, qkv, context, probs, grad_ctx, grads):
            queries, keys_b, values_b = qkv[0], qkv[1], qkv[2]
            upstream = grad_ctx[...]
            delta = jnp.sum(
                upstream.astype(F32) * context[...].astype(F32), axis=0, keepdims=True
            )
            along = dot(values_b, upstream, (0, 0))
            grad_scores = (probs[...].astype(F32) * (along - delta)).astype(BF16)
            grad_q = dot(keys_b, grad_scores, (1, 0)) * scaling
            grad_k = dot(queries, grad_scores, (1, 1)) * scaling
            grad_v = dot(upstream, probs[...], (1, 1))
            grads[0] = grad_q.astype(BF16)
            grads[1] = grad_k.astype(BF16)
            grads[2] = grad_v.astype(BF16)

        (grad_qkv,) = call(
            attend_back_body,
            (heads,),
            [head3, head1, square, head1],
            [(struct((3, share, padded), BF16), head3)],
            flops=16 * padded * padded * 256 * heads,
            moved=8_000_000,
            far=(3,),
        )(scal, qkv, context, probs, grad_ctx)

        extra = 8

        def back_body(s, w, grads, centred_t, gain, early_sums, *refs):
            pieces, (all_sums, scratch, sums) = refs[:-3], refs[-3:]

            @pl.when(pl.program_id(0) == 0)
            def _():
                sums[...] = jnp.zeros_like(sums)

            upstream = grads[...].reshape(3 * share, LANES)
            back = dot(w[...], upstream, (1, 0))
            scratch[...] = back.astype(BF16)
            hat = back * as_col(as_row(gain))
            product = hat * centred_t[...].astype(F32)
            for k in range(0, LANES, 128):
                sums[:width] += product[:, k : k + 128]
                sums[width:] += back[:, k : k + 128]
            mean_one = jnp.sum(hat, axis=0, keepdims=True) / width
            mean_two = jnp.sum(product, axis=0, keepdims=True) / width
            at = lax.broadcasted_iota(jnp.int32, (extra, LANES), 0)
            high_one = mean_one.astype(BF16).astype(F32)
            high_two = mean_two.astype(BF16).astype(F32)
            means = jnp.where(
                at == 0,
                high_one,
                jnp.where(
                    at == 1,
                    mean_one - high_one,
                    jnp.where(at == 2, high_two, jnp.where(at == 3, mean_two - high_two, 0.0)),
                ),
            ).astype(BF16)
            for piece, count, start in zip(pieces, sizes, starts):
                for k in range(count):
                    first = k * (share + extra)
                    rows = scratch[block_of(s, scattered_at + start + k, share)]
                    piece[first : first + share] = rows
                    piece[first + share : first + share + extra] = means

            @pl.when(pl.program_id(0) == steps - 1)
            def _():
                all_sums[0:4] = early_sums[...]
                all_sums[4:5] = jnp.sum(sums[:width].T, axis=0, keepdims=True) / as_row(gain)
                all_sums[5:6] = jnp.sum(sums[width:].T, axis=0, keepdims=True)
                all_sums[6:8] = jnp.zeros((2, width), F32)

        *one_pieces, own_sums = call(
            back_body,
            (steps,),
            [
                whole((width, 3 * share)),
                pl.BlockSpec((3, share, LANES), lambda i, s: (0, 0, i)),
                lanes_of(width),
                vector,
                whole((4, width)),
            ],
            [
                (struct((n * (share + extra), padded), BF16), lanes_of(n * (share + extra)))
                for n in sizes
            ]
            + [(struct((8, width), F32), whole((8, width)))],
            [pltpu.VMEM((width, LANES), BF16), pltpu.VMEM((2 * width, 128), F32)],
            flops=6 * padded * width * share,
            moved=8_000_000,
        )(scal, w_qkv_n, grad_qkv, centred_t, ln1_gain, norm_sums)
        one_got = scatter(one_pieces)

        sums = own_sums
        for stage in range(len(bits)):
            got = along_route(sums, stage)
            sums = sums + got

        wide = 384
        columns = pl.BlockSpec((padded, wide), lambda i, s: (0, i))
        part_of = lambda j: pl.BlockSpec((None, share, padded), lambda i, s: (j, 0, 0))
        out_columns = lambda n: pl.BlockSpec((n, wide), lambda i, s: (0, i))

        def by_core_body(s, first, second, other, mine, rows):
            for c in (0, 1):

                @pl.when(s[core_at] == c)
                def _():
                    mine[:rows] = (second if c else first).astype(BF16)
                    other[:rows] = (first if c else second).astype(BF16)

        def pair_a_body(s, context, grads_q, grad, first_in, other, mine):
            out = dot(context[...], grad[...], (1, 0))
            by_core_body(s, out, dot(grads_q[...], first_in[...], (1, 0)), other, mine, share)

        a_other, a_mine = call(
            pair_a_body,
            (width // wide,),
            [whole((share, padded)), part_of(0), columns, columns],
            [(struct((share, width), BF16), out_columns(share))] * 2,
            flops=4 * share * padded * width,
            moved=6_000_000,
        )(scal, context, grad_qkv, resid_grad, first_in)

        def pair_b_body(s, grads_q, grads_k, grads_v, first_in, sums, bias_up, other, mine, bias_qv):
            @pl.when(pl.program_id(0) == 0)
            def _():
                bias_qv[...] = jnp.zeros_like(bias_qv)
                for k, ref in enumerate((grads_q, grads_v)):
                    total = jnp.sum(ref[...].astype(F32), axis=1, keepdims=True)
                    bias_qv[:, k * share : (k + 1) * share] = col_as_row(total)

            right = first_in[...]
            by_core_body(
                s, dot(grads_k[...], right, (1, 0)), dot(grads_v[...], right, (1, 0)), other, mine, share
            )
            at = lax.broadcasted_iota(jnp.int32, (8, wide), 0)
            here = pl.ds(pl.multiple_of(pl.program_id(0) * wide, 128), wide)
            rows = jnp.where(
                at == 6, bias_up[...], jnp.where(at == 7, bias_qv[:, here], sums[...])
            ).astype(BF16)
            mine[share:] = rows
            other[share:] = rows

        b_other, b_mine = call(
            pair_b_body,
            (width // wide,),
            [part_of(0), part_of(1), part_of(2), columns, out_columns(8), out_columns(1)],
            [(struct((share + 8, width), BF16), out_columns(share + 8))] * 2,
            [pltpu.VMEM((1, width), F32)],
            flops=4 * share * padded * width,
            moved=6_000_000,
        )(scal, grad_qkv, grad_qkv, grad_qkv, first_in, sums, bias_up_grad)

        share_with_core("pa", a_other, a_mine)
        share_with_core("pb", b_other, b_mine)
        line_total = line_sums(parts, place)
        grad_up = dp_sum("u", turned=True)
        grad_down = dp_sum("d")
        a_first, a_second = by_core("pa")
        b_first, b_second = by_core("pb")
        grad_out = a_first.astype(F32)
        grad_wqkv = jnp.concatenate([a_second, b_first[:share], b_second[:share]], axis=0).astype(F32)
        grad_wqkv = grad_wqkv.reshape(3, share, width).transpose(2, 0, 1)

        def unpack_body(s, rows, gain1, shift1, out, gain2, shift2, down, up, qv):
            values = rows[...].astype(F32)
            for k, ref in enumerate((gain2, shift2, out, down, gain1, shift1)):
                ref[...] = values[k]
            up[...] = values[6, :hidden_size]
            qv[0:1] = values[7:8, :share]
            qv[1:2] = values[7:8, share : 2 * share]

        grad_gain1, grad_shift1, grad_b_out, grad_gain2, grad_shift2, grad_b_down, grad_b_up, grad_qv = call(
            unpack_body,
            (1,),
            [pl.BlockSpec((8, width), lambda i, s: (share // 8, 0))],
            [(struct((width,), F32), vector)] * 6
            + [
                (struct((hidden_size,), F32), whole((hidden_size,))),
                (struct((2, share), F32), whole((2, share))),
            ],
        )(scal, line_total["pb"])

        def final_body(s, *refs):
            one, refs = refs[: len(one_got)], refs[len(one_got) :]
            mlp, refs = refs[: len(mlp_got)], refs[len(mlp_got) :]
            resid, grad_in, centred_t, inv_t, gain, b_down, output, grad, *refs = refs
            scratch_a, scratch_b, scratch_c = refs
            back = one[0][...].astype(F32)
            for ref in one[1:]:
                back = back + ref[...].astype(F32)
            total = mlp[0][...].astype(F32)
            for ref in mlp[1:]:
                total = total + ref[...].astype(F32)
            mean_one = back[share : share + 1] + back[share + 1 : share + 2]
            mean_two = back[share + 2 : share + 3] + back[share + 3 : share + 4]
            mine = pl.ds(pl.multiple_of(s[0] * share, share), share)
            scratch_a[...] = resid[...].astype(F32).T
            scratch_b[...] = grad_in[...].astype(F32).T
            scratch_c[...] = jnp.concatenate(
                [as_row(gain), as_row(b_down), jnp.zeros((6, width), F32)], axis=0
            ).T
            columns = scratch_c[mine]
            output[...] = (scratch_a[mine] + total + columns[:, 1:2]).astype(BF16)
            grad[...] = scratch_b[mine] + inv_t[0:1] * (
                back[:share] * columns[:, 0:1] - mean_one - centred_t[...].astype(F32) * mean_two
            )

        mine_rows = pl.BlockSpec((share, LANES), lambda i, s: (s[0], i))
        output_t, input_grad_t = call(
            final_body,
            (steps,),
            [lanes_of(share + extra)] * len(one_got)
            + [lanes_of(share)] * len(mlp_got)
            + [rows_in, rows_in, mine_rows, lanes_of(8), vector, vector],
            [
                (struct((share, tokens), BF16), lanes_of(share)),
                (struct((share, tokens), F32), lanes_of(share)),
            ],
            [pltpu.VMEM((width, LANES), F32)] * 2 + [pltpu.VMEM((width, 8), F32)],
            flops=20 * padded * share,
            moved=10_000_000,
        )(
            scal,
            *one_got,
            *mlp_got,
            resid,
            resid_grad,
            centred_t,
            inv_t,
            ln1_gain,
            bias_down,
        )
        return (
            output_t.T,
            input_grad_t.T,
            grad_gain1,
            grad_shift1,
            grad_wqkv,
            grad_qv,
            grad_out,
            grad_b_out,
            grad_gain2,
            grad_shift2,
            grad_up,
            grad_b_up,
            grad_down,
            grad_b_down,
        )

    return local


def solution(mesh):
    placed = (
        P(DP, None),
        P(DP, None),
        P(),
        P(),
        P(None, None, TENSOR),
        P(None, TENSOR),
        P(TENSOR, None),
        P(),
        P(),
        P(),
        P(None, TENSOR),
        P(TENSOR),
        P(TENSOR, None),
        P(),
    )
    body = make_local(mesh.shape[TENSOR], mesh.shape[DP])

    return jax.shard_map(
        body,
        mesh=mesh,
        in_specs=placed,
        out_specs=(
            P(DP, TENSOR),
            P(DP, TENSOR),
            P(),
            P(),
            P(None, None, TENSOR),
            P(None, TENSOR),
            P(TENSOR, None),
            P(),
            P(),
            P(),
            P(None, TENSOR),
            P(TENSOR),
            P(TENSOR, None),
            P(),
        ),
        check_vma=False,
    )
```
